32 devices in a mesh: dates: 8 (over z, y), tiles: 4 (over x, core).
Axes of the slice: x: 2, y: 2, z: 4, core: 2. Of those that a mesh axis runs over, the one named last changes fastest.
Arguments:
- observed: float32 [256, 32, 1024], P('dates', None, 'tiles'), may hold values from -12 to 12
- cloud_mask: int32 [256, 32, 1024], P('dates', None, 'tiles'), may hold values from 0 to 3
- diffuse_rows: float32 [32, 1024], P(None, 'tiles'), may hold values from 0.02 to 0.24
- diffuse_cols: float32 [32, 1024], P(None, 'tiles'), may hold values from 0.02 to 0.24
Outputs:
- filled: float32 [256, 32, 1024], P('dates', None, 'tiles')
The draws below stay inside these ranges and needn't reach their ends.
All inputs are finite; a program needn't handle non-finite values.
Results may differ from the reference program's by a relative error of at most 0.0003.
Values sent between devices are 32-bit elements; how exact they have to be, the bound alone decides.
A program may use at most 64 MiB of HBM per device.

```python
import math
import jax
import jax.numpy as jnp

DATES = 256
COLS_DEV = 256
ITERS = 10
STEPS = 4
ROWS = 32
COLS = 1024


def draw_observed(key, part):
    first = jax.random.fold_in(key, 0)
    third = jax.random.fold_in(key, 2)
    fourth = jax.random.fold_in(key, 3)
    fifth = jax.random.fold_in(key, 4)
    rowpos = jnp.arange(ROWS, dtype=jnp.float32)[None, :, None] / ROWS
    colpos = jnp.arange(COLS, dtype=jnp.float32)[None, None, :] / COLS
    timepos = jnp.arange(DATES, dtype=jnp.float32)[:, None, None] / DATES
    amplitude_rows = jax.random.uniform(third, (ROWS,), jnp.float32, 0.0, 2.5)
    block_amplitude = jax.random.uniform(fourth, (COLS // COLS_DEV,), jnp.float32, 0.3, 1.5)
    amplitude_cols = jnp.repeat(block_amplitude, COLS_DEV)
    phase = jax.random.uniform(fifth, (ROWS,), jnp.float32, -math.pi, math.pi)
    seasonal = amplitude_rows[None, :, None] * amplitude_cols[None, None, :] * jnp.sin(2.0 * math.pi * 2.0 * timepos + phase[None, :, None])
    rough = jax.random.normal(first, (DATES, ROWS, COLS), jnp.float32)
    scale = jnp.exp(jnp.log(3.0) * rowpos) * jnp.exp(0.5 * colpos)
    values = rough * scale + seasonal
    return jnp.clip(values, -12.0, 12.0)


def draw_cloud_mask(key, part):
    first, second, third, fourth = jax.random.split(key, 4)
    row_share = jax.random.randint(first, (ROWS,), 5, 71)
    block_share = jax.random.randint(second, (COLS // COLS_DEV,), 5, 71)
    column_share = jnp.repeat(block_share, COLS_DEV)
    cloudy = (row_share[:, None] + column_share[None, :]) // 2
    chance = jax.random.randint(third, (DATES, ROWS, COLS), 0, 100)
    levels = jax.random.randint(fourth, (DATES, ROWS, COLS), 1, 4)
    return jnp.where(chance < cloudy[None], 0, levels).astype(jnp.int32)


def block_levels(key, extent, cuts, smallest, top_value):
    factor_of, own = 1.0, jax.random.fold_in(key, 6)
    for axis_at, shards_of in cuts:
        heights = jnp.exp(jax.random.uniform(jax.random.fold_in(own, axis_at), (shards_of,), jnp.float32, smallest / len(cuts), top_value / len(cuts)))
        factor_of = factor_of * jnp.repeat(heights, extent[axis_at] // shards_of).reshape([-1 if axis == axis_at else 1 for axis in range(len(extent))])
    return factor_of


def setup_inputs(seed: int = 0) -> dict:
    seeds = jax.random.split(jax.random.key(seed), 5)
    observed = draw_observed(jax.random.fold_in(seeds[4], 71), 0)
    cloud_mask = draw_cloud_mask(jax.random.fold_in(seeds[4], 71), 0)
    diffuse_rows = jnp.clip(jnp.exp(math.log(0.24) - 2.4849066 * jax.random.uniform(seeds[2], (ROWS, COLS), jnp.float32) ** block_levels(seeds[2], (ROWS, COLS), ((1, 4),), -0.2, 0.2)), 0.02, 0.24)
    diffuse_cols = jnp.clip(jnp.exp(math.log(0.24) - 2.4849066 * jax.random.uniform(seeds[3], (ROWS, COLS), jnp.float32) ** block_levels(seeds[3], (ROWS, COLS), ((1, 4),), -0.2, 0.2)), 0.02, 0.24)
    return dict(observed=observed, cloud_mask=cloud_mask, diffuse_rows=diffuse_rows, diffuse_cols=diffuse_cols)


smooth_weight = 4.0


def time_operator(values, weights):
    second = values[:-2] - 2.0 * values[1:-1] + values[2:]
    padded = jnp.pad(second, ((2, 2), (0, 0), (0, 0)))
    back = padded[:-2] - 2.0 * padded[1:-1] + padded[2:]
    return weights * values + smooth_weight * back


def reference(observed, cloud_mask, diffuse_rows, diffuse_cols):
    weights = cloud_mask.astype(jnp.float32) / 3.0 + 0.05
    rhs = weights * observed
    smoothed = jnp.zeros_like(rhs)
    residual = rhs
    direction = rhs
    norm_now = jnp.sum(residual * residual)
    for step in range(ITERS):
        image = time_operator(direction, weights)
        alpha = norm_now / jnp.sum(direction * image)
        smoothed = smoothed + alpha * direction
        residual = residual - alpha * image
        fresh = jnp.sum(residual * residual)
        direction = residual + (fresh / norm_now) * direction
        norm_now = fresh
    filled = smoothed
    for step in range(STEPS):
        padded = jnp.pad(filled, ((0, 0), (1, 1), (1, 1)))
        centre = padded[:, 1:-1, 1:-1]
        along_rows = padded[:, 2:, 1:-1] + padded[:, :-2, 1:-1] - 2.0 * centre
        along_cols = padded[:, 1:-1, 2:] + padded[:, 1:-1, :-2] - 2.0 * centre
        filled = filled + diffuse_rows * along_rows + diffuse_cols * along_cols
    return filled
```

```python
import functools

import jax
import jax.numpy as jnp
from jax import lax
from jax.experimental import pallas as pl
from jax.experimental.pallas import tpu as pltpu
from jax.sharding import PartitionSpec as P

ITERS = 10
STEPS = 4
LANES = 128
SUB = 8
ROWS_AT_ONCE = 32

smooth_weight = 4.0
LOW, HIGH = 0.05, 65.05
MID, HALF = (LOW + HIGH) / 2, (HIGH - LOW) / 2
PIVOT_MIN = 0.02
MESH = pl.DeviceIdType.MESH


def kernel(nd, nt, chunks, obs_ref, mask_ref, dr_ref, dc_ref, out_ref, flag_ref,
           basis, weights, pack_out, pack_in, coef_in, coefs, acc_ref, sum_a, sum_b, nu_ref, c_ref, halo_ref,
           halo_send, halo_recv, pack_send, pack_recv, coef_send, coef_recv, a_send, a_recv, b_send, b_recv):
    D, R, C = obs_ref.shape
    RC = R // chunks
    me_d, me_t = lax.axis_index("dates"), lax.axis_index("tiles")
    has_l, has_r = me_d > 0, me_d < nd - 1
    has_w, has_e = me_t > 0, me_t < nt - 1
    mask_l = jnp.where(has_l, 1.0, 0.0).astype(jnp.float32)
    mask_r = jnp.where(has_r, 1.0, 0.0).astype(jnp.float32)

    barrier = pltpu.get_barrier_semaphore()
    for o in range(1, nt):
        pl.semaphore_signal(barrier, inc=1, device_id={"tiles": lax.rem(me_t + o, nt)}, device_id_type=MESH)
    for o in range(1, nd):
        pl.semaphore_signal(barrier, inc=1, device_id={"dates": lax.rem(me_d + o, nd)}, device_id_type=MESH)

    def start_plane(t, _):
        w = mask_ref[t].astype(jnp.float32) / 3.0 + 0.05
        weights[t] = w
        basis[0, t + 2] = w * obs_ref[t]
        return 0

    lax.fori_loop(0, D, start_plane, 0)

    def clear(ref, ks, at):
        def one(k, _):
            ref[(k,) + at] = jnp.zeros_like(ref[(k,) + at])
            return 0
        lax.fori_loop(0, ks, one, 0)

    @pl.when(jnp.logical_not(has_l))
    def _():
        clear(basis, ITERS, (pl.ds(0, 2),))

    @pl.when(jnp.logical_not(has_r))
    def _():
        clear(basis, ITERS, (pl.ds(D + 2, 2),))

    @pl.when(jnp.logical_not(has_e))
    def _():
        clear(pack_in, ITERS, (0,))
        coef_in[0] = jnp.zeros_like(coef_in[0])

    @pl.when(jnp.logical_not(has_w))
    def _():
        clear(pack_in, ITERS, (1,))
        coef_in[1] = jnp.zeros_like(coef_in[1])

    pl.semaphore_wait(barrier, nt - 1 + nd - 1)

    def halo_copy(k, c, side):
        rows = pl.ds(c * RC, RC)
        if side == 0:
            src, dst, to = basis.at[k, pl.ds(D, 2), rows], basis.at[k, pl.ds(0, 2), rows], me_d + 1
        else:
            src, dst, to = basis.at[k, pl.ds(2, 2), rows], basis.at[k, pl.ds(D + 2, 2), rows], me_d - 1
        return pltpu.make_async_remote_copy(
            src_ref=src, dst_ref=dst, send_sem=halo_send.at[k, c, side], recv_sem=halo_recv.at[k, c, side],
            device_id={"dates": to}, device_id_type=MESH)

    def pack_copy(k, side):
        return pltpu.make_async_remote_copy(
            src_ref=pack_out.at[k, side], dst_ref=pack_in.at[k, side], send_sem=pack_send.at[k, side],
            recv_sem=pack_recv.at[k, side], device_id={"tiles": me_t - 1 if side == 0 else me_t + 1}, device_id_type=MESH)

    def coef_copy(which, side):
        ref = (dr_ref, dc_ref)[which]
        cols = pl.ds(0 if side == 0 else C - LANES, LANES)
        return pltpu.make_async_remote_copy(
            src_ref=ref.at[:, cols], dst_ref=coef_in.at[side, which], send_sem=coef_send.at[side, which],
            recv_sem=coef_recv.at[side, which], device_id={"tiles": me_t - 1 if side == 0 else me_t + 1}, device_id_type=MESH)

    def send_halo(k, c):
        @pl.when(has_r)
        def _():
            halo_copy(k, c, 0).start()

        @pl.when(has_l)
        def _():
            halo_copy(k, c, 1).start()

    def wait_halo(k, c):
        @pl.when(has_l)
        def _():
            halo_copy(k, c, 0).wait_recv()

        @pl.when(has_r)
        def _():
            halo_copy(k, c, 1).wait_recv()

    for c in range(chunks):
        send_halo(0, c)

    @pl.when(has_w)
    def _():
        for which in range(2):
            coef_copy(which, 0).start()

    @pl.when(has_e)
    def _():
        for which in range(2):
            coef_copy(which, 1).start()

    def second(v, j):
        u = v[j] - 2.0 * v[j + 1] + v[j + 2]
        if j < 0:
            u = u * mask_l
        if j >= D - 2:
            u = u * mask_r
        return u

    def next_plane(k, t, rows, v, u, first):
        back = u[t - 2] - 2.0 * u[t - 1] + u[t]
        image = weights[t, rows] * v[t] + smooth_weight * back
        scale = 1.0 if first else 2.0
        new = (scale / HALF) * image - (scale * MID / HALF) * v[t]
        if not first:
            new = new - basis[k - 1, t + 2, rows]
        return new

    edges = sorted({0, 1, D - 2, D - 1})

    def edge_step(k, c, first):
        def part(r, _):
            rows = pl.ds(pl.multiple_of(c * RC + r * SUB, SUB), SUB)
            v, u = {}, {}
            for t in edges:
                for j in range(t - 2, t + 3):
                    if j not in v:
                        v[j] = basis[k, j + 2, rows]
                for j in range(t - 2, t + 1):
                    if j not in u:
                        u[j] = second(v, j)
                basis[k + 1, t + 2, rows] = next_plane(k, t, rows, v, u, first)
            return 0
        if RC == SUB:
            part(0, 0)
        else:
            lax.fori_loop(0, RC // SUB, part, 0)

    def inner_step(k, first, last):
        def part(r, carry):
            own, cross = carry
            rows = pl.ds(pl.multiple_of(r * SUB, SUB), SUB)
            v, u = {}, {}
            for t in range(D):
                stored = t in edges and not last
                for j in range(t - 2, t + 3):
                    if j not in v and not (stored and j != t):
                        v[j] = basis[k, j + 2, rows]
                if stored:
                    new = basis[k + 1, t + 2, rows]
                else:
                    for j in range(t - 2, t + 1):
                        if j not in u:
                            u[j] = second(v, j)
                    new = next_plane(k, t, rows, v, u, first)
                    if not last:
                        basis[k + 1, t + 2, rows] = new
                own = own + v[t] * v[t]
                cross = cross + v[t] * new
            return own, cross
        zero = jnp.zeros((SUB, C), jnp.float32)
        own, cross = lax.fori_loop(0, R // SUB, part, (zero, zero))
        for which, acc in ((0, own), (1, cross)):
            acc_ref[k, which] = functools.reduce(lambda a, b: a + b, [acc[:, i:i + LANES] for i in range(0, C, LANES)])

    lane = lax.broadcasted_iota(jnp.int32, (ROWS_AT_ONCE, LANES), 1)
    group = lane // STEPS
    groups = LANES // STEPS

    def pack_step(k):
        def part(r, _):
            rows = pl.ds(pl.multiple_of(r * ROWS_AT_ONCE, ROWS_AT_ONCE), ROWS_AT_ONCE)
            west = east = jnp.zeros((ROWS_AT_ONCE, LANES), jnp.float32)
            for d in range(D):
                both = jnp.where(lane < LANES // 2, basis[k, d + 2, rows, pl.ds(0, LANES)],
                                 basis[k, d + 2, rows, pl.ds(C - LANES, LANES)])
                if d:
                    both = pltpu.roll(both, STEPS * d, 1)
                west = jnp.where(group == d, both, west)
                east = jnp.where(group == (d - 1) % groups, both, east)
            pack_out[k, 0, rows] = west
            pack_out[k, 1, rows] = east
            return 0
        lax.fori_loop(0, R // ROWS_AT_ONCE, part, 0)

        @pl.when(has_w)
        def _():
            pack_copy(k, 0).start()

        @pl.when(has_e)
        def _():
            pack_copy(k, 1).start()

    def step(k, first=False, last=False):
        if last:
            pack_step(k)
        for c in range(chunks):
            wait_halo(k, c)
            if not last:
                edge_step(k, c, first)
                send_halo(k + 1, c)
        inner_step(k, first, last)
        if not last:
            pack_step(k)

    step(0, first=True)

    def middle(k, _):
        step(k)
        return 0

    lax.fori_loop(1, ITERS - 1, middle, 0)
    step(ITERS - 1, last=True)

    def exchange(ref, value, axis, me, count, send, recv):
        ref[me] = value
        def copy(o, slot):
            return pltpu.make_async_remote_copy(
                src_ref=ref.at[me], dst_ref=ref.at[me] if slot is None else ref.at[slot],
                send_sem=send.at[o], recv_sem=recv.at[me] if slot is None else recv.at[slot],
                device_id={axis: lax.rem(me + o, count)}, device_id_type=MESH)
        for o in range(1, count):
            copy(o, None).start()
        for o in range(1, count):
            copy(o, lax.rem(me + o, count)).wait_recv()
        total = ref[0]
        for j in range(1, count):
            total = total + ref[j]
        for o in range(1, count):
            copy(o, None).wait_send()
        return total

    n_mom = 2 * ITERS
    mine = jnp.sum(acc_ref[...].reshape(n_mom, SUB, LANES), axis=1)
    mine = jnp.concatenate([mine, jnp.zeros((sum_a.shape[1] - n_mom, LANES), jnp.float32)], axis=0)
    total = exchange(sum_a, mine, "tiles", me_t, nt, a_send, a_recv)
    total = exchange(sum_b, total, "dates", me_d, nd, b_send, b_recv)
    nu_ref[...] = jnp.broadcast_to(jnp.sum(total, axis=1, keepdims=True), nu_ref.shape)

    raw = [jnp.broadcast_to(nu_ref[j:j + 1, :], (SUB, LANES)) for j in range(n_mom)]
    unit = 1.0 / raw[0]
    raw = [value * unit for value in raw]
    nu = raw[:2]
    for k in range(1, ITERS):
        nu += [2.0 * raw[2 * k] - nu[0], 2.0 * raw[2 * k + 1] - nu[1]]
    h = [MID * nu[m] + (HALF * 0.5) * (nu[m + 1] + nu[abs(m - 1)]) for m in range(n_mom - 1)]
    M = {(i, j): 0.5 * (h[i + j] + h[j - i]) for i in range(ITERS) for j in range(i, ITERS)}
    b = list(nu[:ITERS])
    size = [M[i, i] for i in range(ITERS)]
    inverse, worst = [], None
    for i in range(ITERS):
        inverse.append(1.0 / M[i, i])
        ratio = jnp.where(M[i, i] > PIVOT_MIN * size[i], 1.0, 0.0)
        worst = ratio if worst is None else worst * ratio
        for j in range(i + 1, ITERS):
            f = M[i, j] * inverse[i]
            for q in range(j, ITERS):
                M[j, q] = M[j, q] - f * M[i, q]
            b[j] = b[j] - f * b[i]
    coef = [None] * ITERS
    for i in reversed(range(ITERS)):
        s = b[i]
        for q in range(i + 1, ITERS):
            s = s - M[i, q] * coef[q]
        coef[i] = s * inverse[i]
        c_ref[i] = coef[i]
    flag_ref[...] = worst

    for side, has in ((0, has_e), (1, has_w)):
        @pl.when(has)
        def _():
            for which in range(2):
                coef_copy(which, side).wait_recv()

            def one(k, _):
                pack_copy(k, side).wait_recv()
                return 0
            lax.fori_loop(0, ITERS, one, 0)

    wide = lax.broadcasted_iota(jnp.int32, (R, LANES), 1)
    is_e, is_w = wide < STEPS, wide >= LANES - STEPS

    def widened(ref, which):
        ends = jnp.where(is_e, coef_in[0, which], jnp.where(is_w, coef_in[1, which], 0.0))
        return jnp.concatenate([ref[...], ends], axis=1)

    dr, dc = widened(dr_ref, 0), widened(dc_ref, 1)
    row = lax.broadcasted_iota(jnp.int32, dr.shape, 0)
    coefs[0] = jnp.where(row > 0, dr, 0.0)
    coefs[1] = jnp.where(row < R - 1, dr, 0.0)
    coefs[2] = dc
    coefs[3] = 1.0 - 2.0 * dr - 2.0 * dc

    cs = [c_ref[i, 0:1, :] for i in range(ITERS)]
    for side in range(2):
        halo_ref[side] = functools.reduce(lambda a, b: a + b, [cs[i] * pack_in[i, side] for i in range(ITERS)])

    width = C + LANES

    def diffuse(d, _):
        parts = []
        for i in range(0, C, LANES):
            parts.append(functools.reduce(
                lambda a, b: a + b, [c_ref[k, 0:1, :] * basis[k, d + 2, :, pl.ds(i, LANES)] for k in range(ITERS)]))
        ends = jnp.where(wide // STEPS == d, halo_ref[0], halo_ref[1])
        ends = pltpu.roll(ends, lax.rem(LANES - STEPS * d, LANES), 1)
        parts.append(jnp.where(jnp.logical_or(is_e, is_w), ends, 0.0))
        f = jnp.concatenate(parts, axis=1)
        for _ in range(STEPS):
            f = (coefs[3] * f + coefs[0] * pltpu.roll(f, 1, 0) + coefs[1] * pltpu.roll(f, R - 1, 0)
                 + coefs[2] * (pltpu.roll(f, 1, 1) + pltpu.roll(f, width - 1, 1)))
        out_ref[d] = f[:, :C]
        return 0

    lax.fori_loop(0, D, diffuse, 0)

    def sent(k, _):
        for side, has, has_t in ((0, has_r, has_w), (1, has_l, has_e)):
            @pl.when(has)
            def _():
                for c in range(chunks):
                    halo_copy(k, c, side).wait_send()

            @pl.when(has_t)
            def _():
                pack_copy(k, side).wait_send()
        return 0

    lax.fori_loop(0, ITERS, sent, 0)
    for side, has in ((0, has_w), (1, has_e)):
        @pl.when(has)
        def _():
            for which in range(2):
                coef_copy(which, side).wait_send()


def fast(nd, nt, observed, cloud_mask, diffuse_rows, diffuse_cols):
    D, R, C = observed.shape
    chunks = 4
    slots = 24
    f32 = jnp.float32
    DMA = pltpu.SemaphoreType.DMA
    V = pl.BlockSpec(memory_space=pltpu.VMEM)
    return pl.pallas_call(
        functools.partial(kernel, nd, nt, chunks),
        out_shape=(jax.ShapeDtypeStruct((D, R, C), f32), jax.ShapeDtypeStruct((SUB, LANES), f32)),
        in_specs=[V] * 4,
        out_specs=(V, V),
        scratch_shapes=[
            pltpu.VMEM((ITERS, D + 4, R, C), f32),
            pltpu.VMEM((D, R, C), f32),
            pltpu.VMEM((ITERS, 2, R, LANES), f32),
            pltpu.VMEM((ITERS, 2, R, LANES), f32),
            pltpu.VMEM((2, 2, R, LANES), f32),
            pltpu.VMEM((4, R, C + LANES), f32),
            pltpu.VMEM((ITERS, 2, SUB, LANES), f32),
            pltpu.VMEM((nt, slots, LANES), f32),
            pltpu.VMEM((nd, slots, LANES), f32),
            pltpu.VMEM((slots, LANES), f32),
            pltpu.VMEM((ITERS, SUB, LANES), f32),
            pltpu.VMEM((2, R, LANES), f32),
            DMA((ITERS, chunks, 2)), DMA((ITERS, chunks, 2)),
            DMA((ITERS, 2)), DMA((ITERS, 2)),
            DMA((2, 2)), DMA((2, 2)),
            DMA((nt,)), DMA((nt,)),
            DMA((nd,)), DMA((nd,)),
        ],
        compiler_params=pltpu.CompilerParams(
            collective_id=0, has_side_effects=True, vmem_limit_bytes=60 * 1024 * 1024),
        name="smooth_and_fill",
    )(observed, cloud_mask, diffuse_rows, diffuse_cols)


def padded_by(cells, axis, dim, width):
    count = lax.axis_size(axis)
    head = lax.slice_in_dim(cells, 0, width, axis=dim)
    tail = lax.slice_in_dim(cells, cells.shape[dim] - width, cells.shape[dim], axis=dim)
    return jnp.concatenate(
        [
            lax.ppermute(tail, axis, [(i, i + 1) for i in range(count - 1)]),
            cells,
            lax.ppermute(head, axis, [(i + 1, i) for i in range(count - 1)]),
        ],
        axis=dim,
    )


def total_of(value):
    for axis in ("tiles", "dates"):
        count = lax.axis_size(axis)
        shift = 1
        while shift < count:
            value = value + lax.ppermute(value, axis, [(i, i ^ shift) for i in range(count)])
            shift *= 2
    return value


def plain(observed, cloud_mask, diffuse_rows, diffuse_cols):
    weights = cloud_mask.astype(jnp.float32) / 3.0 + 0.05
    rhs = weights * observed
    D = rhs.shape[0]
    dates = D * lax.axis_size("dates")
    place = lax.axis_index("dates") * D - 2 + jnp.arange(D + 2)
    inside = jnp.logical_and(place >= 0, place < dates - 2)[:, None, None]

    def time_operator(values):
        wide = padded_by(values, "dates", 0, 2)
        second = jnp.where(inside, wide[:-2] - 2.0 * wide[1:-1] + wide[2:], 0.0)
        return weights * values + smooth_weight * (second[:-2] - 2.0 * second[1:-1] + second[2:])

    def advance(step, state):
        smoothed, residual, direction, norm_now = state
        image = time_operator(direction)
        alpha = norm_now / total_of(jnp.sum(direction * image))
        smoothed = smoothed + alpha * direction
        residual = residual - alpha * image
        fresh = total_of(jnp.sum(residual * residual))
        direction = residual + fresh / norm_now * direction
        return (smoothed, residual, direction, fresh)

    state = (jnp.zeros_like(rhs), rhs, rhs, total_of(jnp.sum(rhs * rhs)))
    filled = lax.fori_loop(0, ITERS, advance, state)[0]

    def spread(step, filled):
        padded = jnp.pad(padded_by(filled, "tiles", 2, 1), ((0, 0), (1, 1), (0, 0)))
        centre = padded[:, 1:-1, 1:-1]
        along_rows = padded[:, 2:, 1:-1] + padded[:, :-2, 1:-1] - 2.0 * centre
        along_cols = padded[:, 1:-1, 2:] + padded[:, 1:-1, :-2] - 2.0 * centre
        return filled + diffuse_rows * along_rows + diffuse_cols * along_cols

    return lax.fori_loop(0, STEPS, spread, filled)


def solution(mesh):
    nd, nt = mesh.shape["dates"], mesh.shape["tiles"]

    def body(observed, cloud_mask, diffuse_rows, diffuse_cols):
        filled, good = fast(nd, nt, observed, cloud_mask, diffuse_rows, diffuse_cols)
        return lax.cond(
            good[0, 0] > 0.5,
            lambda: filled,
            lambda: plain(observed, cloud_mask, diffuse_rows, diffuse_cols),
        )

    in_specs = (
        P("dates", None, "tiles"),
        P("dates", None, "tiles"),
        P(None, "tiles"),
        P(None, "tiles"),
    )
    return jax.shard_map(body, mesh=mesh, in_specs=in_specs, out_specs=P("dates", None, "tiles"), check_vma=False)
```

```python
import functools

import jax
import jax.numpy as jnp
from jax import lax
from jax.experimental import pallas as pl
from jax.experimental.pallas import tpu as pltpu
from jax.sharding import PartitionSpec as P

ITERS = 10
STEPS = 4
LANES = 128
SUB = 8

smooth_weight = 4.0
LOW, HIGH = 0.05, 65.05
MID, HALF = (LOW + HIGH) / 2, (HIGH - LOW) / 2
PIVOT_MIN = 0.02
MESH = pl.DeviceIdType.MESH


def kernel(nd, nt, row_chunks, col_chunks, obs_ref, mask_ref, dr_ref, dc_ref, out_ref, flag_ref,
           basis, weights, pack_out, pack_in, coef_in, coefs, acc_ref, sum_a, sum_b, nu_ref, c_ref, halo_ref,
           halo_send, halo_recv, pack_send, pack_recv, coef_send, coef_recv, a_send, a_recv, b_send, b_recv):
    D, R, C = obs_ref.shape
    chunks = row_chunks * col_chunks
    RC, CC = R // row_chunks, C // col_chunks
    me_d, me_t = lax.axis_index("dates"), lax.axis_index("tiles")
    has_l, has_r = me_d > 0, me_d < nd - 1
    has_w, has_e = me_t > 0, me_t < nt - 1
    mask_l = jnp.where(has_l, 1.0, 0.0).astype(jnp.float32)
    mask_r = jnp.where(has_r, 1.0, 0.0).astype(jnp.float32)

    barrier = pltpu.get_barrier_semaphore()
    for o in range(1, nt):
        pl.semaphore_signal(barrier, inc=1, device_id={"tiles": lax.rem(me_t + o, nt)}, device_id_type=MESH)
    greeted = (1, nd - 1) if 2 < nd < ITERS else range(1, nd)
    for o in greeted:
        pl.semaphore_signal(barrier, inc=1, device_id={"dates": lax.rem(me_d + o, nd)}, device_id_type=MESH)

    def start_plane(t, _):
        w = mask_ref[t].astype(jnp.float32) / 3.0 + 0.05
        weights[t] = w
        basis[0, t + 2] = w * obs_ref[t]
        return 0

    edges = sorted({0, 1, D - 2, D - 1})
    for t in edges:
        start_plane(t, 0)

    pl.semaphore_wait(barrier, nt - 1 + len(greeted))

    def halo_copy(k, c, side):
        rows, cols = pl.ds(c // col_chunks * RC, RC), pl.ds(c % col_chunks * CC, CC)
        if side == 0:
            src, dst, to = basis.at[k, pl.ds(D, 2), rows, cols], basis.at[k, pl.ds(0, 2), rows, cols], me_d + 1
        else:
            src, dst, to = basis.at[k, pl.ds(2, 2), rows, cols], basis.at[k, pl.ds(D + 2, 2), rows, cols], me_d - 1
        return pltpu.make_async_remote_copy(
            src_ref=src, dst_ref=dst, send_sem=halo_send.at[k, c, side], recv_sem=halo_recv.at[k, c, side],
            device_id={"dates": to}, device_id_type=MESH)

    def pack_copy(k, side):
        return pltpu.make_async_remote_copy(
            src_ref=pack_out.at[k, side], dst_ref=pack_in.at[k, side], send_sem=pack_send.at[k, side],
            recv_sem=pack_recv.at[k, side], device_id={"tiles": me_t - 1 if side == 0 else me_t + 1}, device_id_type=MESH)

    def coef_copy(which, side):
        ref = (dr_ref, dc_ref)[which]
        cols = pl.ds(0 if side == 0 else C - LANES, LANES)
        return pltpu.make_async_remote_copy(
            src_ref=ref.at[:, cols], dst_ref=coef_in.at[side, which], send_sem=coef_send.at[side, which],
            recv_sem=coef_recv.at[side, which], device_id={"tiles": me_t - 1 if side == 0 else me_t + 1}, device_id_type=MESH)

    def send_halo(k, c, both=True):
        @pl.when(has_r)
        def _():
            halo_copy(k, c, 0).start()

        if both:
            @pl.when(has_l)
            def _():
                halo_copy(k, c, 1).start()

    def wait_halo(k, c, both=True):
        @pl.when(has_l)
        def _():
            halo_copy(k, c, 0).wait_recv()

        if both:
            @pl.when(has_r)
            def _():
                halo_copy(k, c, 1).wait_recv()

    for c in range(chunks):
        send_halo(0, c)

    @pl.when(has_w)
    def _():
        for which in range(2):
            coef_copy(which, 0).start()

    @pl.when(has_e)
    def _():
        for which in range(2):
            coef_copy(which, 1).start()

    lax.fori_loop(2, D - 2, start_plane, 0)

    def clear(ref, ks, at):
        def one(k, _):
            ref[(k,) + at] = jnp.zeros_like(ref[(k,) + at])
            return 0
        lax.fori_loop(0, ks, one, 0)

    @pl.when(jnp.logical_not(has_l))
    def _():
        clear(basis, ITERS, (pl.ds(0, 2),))

    @pl.when(jnp.logical_not(has_r))
    def _():
        clear(basis, ITERS, (pl.ds(D + 2, 2),))

    @pl.when(jnp.logical_not(has_e))
    def _():
        clear(pack_in, ITERS, (0,))
        coef_in[0] = jnp.zeros_like(coef_in[0])

    @pl.when(jnp.logical_not(has_w))
    def _():
        clear(pack_in, ITERS, (1,))
        coef_in[1] = jnp.zeros_like(coef_in[1])

    def second(v, j):
        u = v[j] - 2.0 * v[j + 1] + v[j + 2]
        if j < 0:
            u = u * mask_l
        if j >= D - 2:
            u = u * mask_r
        return u

    def next_plane(k, t, rows, cols, v, u, first):
        back = u[t - 2] - 2.0 * u[t - 1] + u[t]
        image = weights[t, rows, cols] * v[t] + smooth_weight * back
        scale = 1.0 if first else 2.0
        new = (scale / HALF) * image - (scale * MID / HALF) * v[t]
        if not first:
            new = new - basis[k - 1, t + 2, rows, cols]
        return new

    def place(c, r):
        return (pl.ds(pl.multiple_of(c // col_chunks * RC + r * SUB, SUB), SUB), pl.ds(c % col_chunks * CC, CC))

    def edge_step(k, c, first):
        def part(r, _):
            rows, cols = place(c, r)
            v, u = {}, {}
            for t in edges:
                for j in range(t - 2, t + 3):
                    if j not in v:
                        v[j] = basis[k, j + 2, rows, cols]
                for j in range(t - 2, t + 1):
                    if j not in u:
                        u[j] = second(v, j)
                basis[k + 1, t + 2, rows, cols] = next_plane(k, t, rows, cols, v, u, first)
            return 0
        if RC == SUB:
            part(0, 0)
        else:
            lax.fori_loop(0, RC // SUB, part, 0)

    def inner_step(k, c, first, last):
        def part(r, carry):
            own, cross = carry
            rows, cols = place(c, r)
            v, u = {}, {}
            for t in range(D):
                stored = t in edges
                for j in range(t - 2, t + 3):
                    if j not in v and not (stored and j != t):
                        v[j] = basis[k, j + 2, rows, cols]
                if stored:
                    new = basis[k + 1, t + 2, rows, cols]
                else:
                    for j in range(t - 2, t + 1):
                        if j not in u:
                            u[j] = second(v, j)
                    new = next_plane(k, t, rows, cols, v, u, first)
                    basis[k + 1, t + 2, rows, cols] = new
                own = own + v[t] * v[t]
                cross = cross + v[t] * new
            return own, cross

        def last_part(r, carry):
            own, energy = carry
            rows, cols = place(c, r)
            v = {j: basis[k, j + 2, rows, cols] for j in range(-2, D)}
            bend = jnp.zeros_like(own)
            for t in range(D):
                u = second(v, t - 2)
                bend = bend + u * u
                square = v[t] * v[t]
                own = own + square
                energy = energy + weights[t, rows, cols] * square
            return own, energy + smooth_weight * bend

        if last:
            part = last_part
        zero = jnp.zeros((SUB, CC), jnp.float32)
        own, cross = part(0, (zero, zero)) if RC == SUB else lax.fori_loop(0, RC // SUB, part, (zero, zero))
        for which, acc in ((0, own), (1, cross)):
            acc = functools.reduce(lambda a, b: a + b, [acc[:, i:i + LANES] for i in range(0, CC, LANES)])
            acc_ref[k, which] = acc if c == 0 else acc_ref[k, which] + acc

    lane = lax.broadcasted_iota(jnp.int32, (SUB, LANES), 1)
    group = lane // STEPS
    groups = LANES // STEPS

    def pack_step(k, c):
        def part(r, _):
            rows = pl.ds(pl.multiple_of(c * RC + r * SUB, SUB), SUB)
            west = east = jnp.zeros((SUB, LANES), jnp.float32)
            for d in range(D):
                both = jnp.where(lane < LANES // 2, basis[k, d + 2, rows, pl.ds(0, LANES)],
                                 basis[k, d + 2, rows, pl.ds(C - LANES, LANES)])
                if d:
                    both = pltpu.roll(both, STEPS * d, 1)
                west = jnp.where(group == d, both, west)
                east = jnp.where(group == (d - 1) % groups, both, east)
            pack_out[k, 0, rows] = west
            pack_out[k, 1, rows] = east
            return 0
        if RC == SUB:
            part(0, 0)
        else:
            lax.fori_loop(0, RC // SUB, part, 0)

    def send_pack(k):
        @pl.when(has_w)
        def _():
            pack_copy(k, 0).start()

        @pl.when(has_e)
        def _():
            pack_copy(k, 1).start()

    def step(k, first=False, last=False, before_last=False):
        if last:
            for c in range(row_chunks):
                pack_step(k, c)
            send_pack(k)
        for c in range(chunks):
            wait_halo(k, c, not last)
            if not last:
                edge_step(k, c, first)
                send_halo(k + 1, c, not before_last)
            inner_step(k, c, first, last)
            if not last and c % col_chunks == col_chunks - 1:
                pack_step(k, c // col_chunks)
        if not last:
            send_pack(k)

    step(0, first=True)

    def middle(k, _):
        step(k)
        return 0

    lax.fori_loop(1, ITERS - 2, middle, 0)
    step(ITERS - 2, before_last=True)
    step(ITERS - 1, last=True)

    def exchange(ref, value, axis, me, count, send, recv, meanwhile):
        ref[me] = value
        def copy(o, slot):
            return pltpu.make_async_remote_copy(
                src_ref=ref.at[me], dst_ref=ref.at[me] if slot is None else ref.at[slot],
                send_sem=send.at[o], recv_sem=recv.at[me] if slot is None else recv.at[slot],
                device_id={axis: lax.rem(me + o, count)}, device_id_type=MESH)
        for o in range(1, count):
            copy(o, None).start()
        meanwhile()
        for o in range(1, count):
            copy(o, lax.rem(me + o, count)).wait_recv()
        total = ref[0]
        for j in range(1, count):
            total = total + ref[j]
        for o in range(1, count):
            copy(o, None).wait_send()
        return total

    wide = lax.broadcasted_iota(jnp.int32, (R, LANES), 1)
    is_e, is_w = wide < STEPS, wide >= LANES - STEPS

    def ready():
        for side, has in ((0, has_e), (1, has_w)):
            @pl.when(has)
            def _():
                for which in range(2):
                    coef_copy(which, side).wait_recv()

                def one(k, _):
                    pack_copy(k, side).wait_recv()
                    return 0
                lax.fori_loop(0, ITERS, one, 0)

        def widened(ref, which):
            ends = jnp.where(is_e, coef_in[0, which], jnp.where(is_w, coef_in[1, which], 0.0))
            return jnp.concatenate([ref[...], ends], axis=1)

        dr, dc = widened(dr_ref, 0), widened(dc_ref, 1)
        row = lax.broadcasted_iota(jnp.int32, dr.shape, 0)
        coefs[0] = jnp.where(row > 0, dr, 0.0)
        coefs[1] = jnp.where(row < R - 1, dr, 0.0)
        coefs[2] = dc
        coefs[3] = 1.0 - 2.0 * dr - 2.0 * dc

    def drained():
        def sent(k, _):
            for side, has, has_t in ((0, has_r, has_w), (1, has_l, has_e)):
                @pl.when(has if side == 0 else jnp.logical_and(has, k < ITERS - 1))
                def _():
                    for c in range(chunks):
                        halo_copy(k, c, side).wait_send()

                @pl.when(has_t)
                def _():
                    pack_copy(k, side).wait_send()
            return 0

        lax.fori_loop(0, ITERS, sent, 0)
        for side, has in ((0, has_w), (1, has_e)):
            @pl.when(has)
            def _():
                for which in range(2):
                    coef_copy(which, side).wait_send()

    n_mom = 2 * ITERS
    mine = jnp.sum(acc_ref[...].reshape(n_mom, SUB, LANES), axis=1)
    mine = jnp.concatenate([mine, jnp.zeros((sum_a.shape[1] - n_mom, LANES), jnp.float32)], axis=0)
    total = exchange(sum_a, mine, "tiles", me_t, nt, a_send, a_recv, ready)
    total = exchange(sum_b, total, "dates", me_d, nd, b_send, b_recv, drained)
    nu_ref[...] = jnp.broadcast_to(jnp.sum(total, axis=1, keepdims=True), nu_ref.shape)

    raw = [jnp.broadcast_to(nu_ref[j:j + 1, :], (SUB, LANES)) for j in range(n_mom)]
    unit = 1.0 / raw[0]
    raw = [value * unit for value in raw]
    raw[-1] = (2.0 / HALF) * (raw[-1] - MID * raw[-2]) - raw[-3]
    nu = raw[:2]
    for k in range(1, ITERS):
        nu += [2.0 * raw[2 * k] - nu[0], 2.0 * raw[2 * k + 1] - nu[1]]
    h = [MID * nu[m] + (HALF * 0.5) * (nu[m + 1] + nu[abs(m - 1)]) for m in range(n_mom - 1)]
    M = {(i, j): 0.5 * (h[i + j] + h[j - i]) for i in range(ITERS) for j in range(i, ITERS)}
    b = list(nu[:ITERS])
    size = [M[i, i] for i in range(ITERS)]
    inverse, worst = [], None
    for i in range(ITERS):
        inverse.append(1.0 / M[i, i])
        ratio = jnp.where(M[i, i] > PIVOT_MIN * size[i], 1.0, 0.0)
        worst = ratio if worst is None else worst * ratio
        for j in range(i + 1, ITERS):
            f = M[i, j] * inverse[i]
            for q in range(j, ITERS):
                M[j, q] = M[j, q] - f * M[i, q]
            b[j] = b[j] - f * b[i]
    coef = [None] * ITERS
    for i in reversed(range(ITERS)):
        s = b[i]
        for q in range(i + 1, ITERS):
            s = s - M[i, q] * coef[q]
        coef[i] = s * inverse[i]
        c_ref[i] = coef[i]
    flag_ref[0] = jnp.min(worst)

    cs = [c_ref[i, 0:1, :] for i in range(ITERS)]
    for side in range(2):
        halo_ref[side] = functools.reduce(lambda a, b: a + b, [cs[i] * pack_in[i, side] for i in range(ITERS)])

    width = C + LANES

    def diffuse(d, _):
        parts = []
        for i in range(0, C, LANES):
            parts.append(functools.reduce(
                lambda a, b: a + b, [c_ref[k, 0:1, :] * basis[k, d + 2, :, pl.ds(i, LANES)] for k in range(ITERS)]))
        ends = jnp.where(wide // STEPS == d, halo_ref[0], halo_ref[1])
        ends = pltpu.roll(ends, lax.rem(LANES - STEPS * d, LANES), 1)
        parts.append(jnp.where(jnp.logical_or(is_e, is_w), ends, 0.0))
        f = jnp.concatenate(parts, axis=1)
        for _ in range(STEPS):
            f = (coefs[3] * f + coefs[0] * pltpu.roll(f, 1, 0) + coefs[1] * pltpu.roll(f, R - 1, 0)
                 + coefs[2] * (pltpu.roll(f, 1, 1) + pltpu.roll(f, width - 1, 1)))
        out_ref[d] = f[:, :C]
        return 0

    lax.fori_loop(0, D, diffuse, 0, unroll=4 if D * R <= 1024 else 1)


def fast(nd, nt, observed, cloud_mask, diffuse_rows, diffuse_cols):
    D, R, C = observed.shape
    row_chunks, col_chunks = 4, 1
    chunks = row_chunks * col_chunks
    slots = 24
    f32 = jnp.float32
    DMA = pltpu.SemaphoreType.DMA
    V = pl.BlockSpec(memory_space=pltpu.VMEM)
    return pl.pallas_call(
        functools.partial(kernel, nd, nt, row_chunks, col_chunks),
        out_shape=(jax.ShapeDtypeStruct((D, R, C), f32), jax.ShapeDtypeStruct((1,), f32)),
        in_specs=[V] * 4,
        out_specs=(V, pl.BlockSpec(memory_space=pltpu.SMEM)),
        scratch_shapes=[
            pltpu.VMEM((ITERS, D + 4, R, C), f32),
            pltpu.VMEM((D, R, C), f32),
            pltpu.VMEM((ITERS, 2, R, LANES), f32),
            pltpu.VMEM((ITERS, 2, R, LANES), f32),
            pltpu.VMEM((2, 2, R, LANES), f32),
            pltpu.VMEM((4, R, C + LANES), f32),
            pltpu.VMEM((ITERS, 2, SUB, LANES), f32),
            pltpu.VMEM((nt, slots, LANES), f32),
            pltpu.VMEM((nd, slots, LANES), f32),
            pltpu.VMEM((slots, LANES), f32),
            pltpu.VMEM((ITERS, SUB, LANES), f32),
            pltpu.VMEM((2, R, LANES), f32),
            DMA((ITERS, chunks, 2)), DMA((ITERS, chunks, 2)),
            DMA((ITERS, 2)), DMA((ITERS, 2)),
            DMA((2, 2)), DMA((2, 2)),
            DMA((nt,)), DMA((nt,)),
            DMA((nd,)), DMA((nd,)),
        ],
        compiler_params=pltpu.CompilerParams(
            collective_id=0, has_side_effects=True, vmem_limit_bytes=60 * 1024 * 1024),
        name="smooth_and_fill",
    )(observed, cloud_mask, diffuse_rows, diffuse_cols)


def padded_by(cells, axis, dim, width):
    count = lax.axis_size(axis)
    head = lax.slice_in_dim(cells, 0, width, axis=dim)
    tail = lax.slice_in_dim(cells, cells.shape[dim] - width, cells.shape[dim], axis=dim)
    return jnp.concatenate(
        [
            lax.ppermute(tail, axis, [(i, i + 1) for i in range(count - 1)]),
            cells,
            lax.ppermute(head, axis, [(i + 1, i) for i in range(count - 1)]),
        ],
        axis=dim,
    )


def total_of(value):
    for axis in ("tiles", "dates"):
        count = lax.axis_size(axis)
        shift = 1
        while shift < count:
            value = value + lax.ppermute(value, axis, [(i, i ^ shift) for i in range(count)])
            shift *= 2
    return value


def plain(observed, cloud_mask, diffuse_rows, diffuse_cols):
    weights = cloud_mask.astype(jnp.float32) / 3.0 + 0.05
    rhs = weights * observed
    D = rhs.shape[0]
    dates = D * lax.axis_size("dates")
    place = lax.axis_index("dates") * D - 2 + jnp.arange(D + 2)
    inside = jnp.logical_and(place >= 0, place < dates - 2)[:, None, None]

    def time_operator(values):
        wide = padded_by(values, "dates", 0, 2)
        second = jnp.where(inside, wide[:-2] - 2.0 * wide[1:-1] + wide[2:], 0.0)
        return weights * values + smooth_weight * (second[:-2] - 2.0 * second[1:-1] + second[2:])

    def advance(step, state):
        smoothed, residual, direction, norm_now = state
        image = time_operator(direction)
        alpha = norm_now / total_of(jnp.sum(direction * image))
        smoothed = smoothed + alpha * direction
        residual = residual - alpha * image
        fresh = total_of(jnp.sum(residual * residual))
        direction = residual + fresh / norm_now * direction
        return (smoothed, residual, direction, fresh)

    state = (jnp.zeros_like(rhs), rhs, rhs, total_of(jnp.sum(rhs * rhs)))
    filled = lax.fori_loop(0, ITERS, advance, state)[0]

    def spread(step, filled):
        padded = jnp.pad(padded_by(filled, "tiles", 2, 1), ((0, 0), (1, 1), (0, 0)))
        centre = padded[:, 1:-1, 1:-1]
        along_rows = padded[:, 2:, 1:-1] + padded[:, :-2, 1:-1] - 2.0 * centre
        along_cols = padded[:, 1:-1, 2:] + padded[:, 1:-1, :-2] - 2.0 * centre
        return filled + diffuse_rows * along_rows + diffuse_cols * along_cols

    return lax.fori_loop(0, STEPS, spread, filled)


def solution(mesh):
    nd, nt = mesh.shape["dates"], mesh.shape["tiles"]

    def body(observed, cloud_mask, diffuse_rows, diffuse_cols):
        filled, good = fast(nd, nt, observed, cloud_mask, diffuse_rows, diffuse_cols)
        return lax.cond(
            good[0] > 0.5,
            lambda: filled,
            lambda: plain(observed, cloud_mask, diffuse_rows, diffuse_cols),
        )

    in_specs = (
        P("dates", None, "tiles"),
        P("dates", None, "tiles"),
        P(None, "tiles"),
        P(None, "tiles"),
    )
    return jax.shard_map(body, mesh=mesh, in_specs=in_specs, out_specs=P("dates", None, "tiles"), check_vma=False)
```

```python
import functools

import jax
import jax.numpy as jnp
from jax import lax
from jax.experimental import pallas as pl
from jax.experimental.pallas import tpu as pltpu
from jax.sharding import PartitionSpec as P

ITERS = 10
STEPS = 4
LANES = 128
SUB = 8

smooth_weight = 4.0
LOW, HIGH = 0.05, 65.05
MID, HALF = (LOW + HIGH) / 2, (HIGH - LOW) / 2
PIVOT_MIN = 0.02
MESH = pl.DeviceIdType.MESH


def kernel(nd, nt, row_chunks, col_chunks, obs_ref, mask_ref, dr_ref, dc_ref, out_ref, flag_ref,
           basis, weights, pack_out, pack_in, coef_in, coefs, acc_ref, sum_a, sum_b, nu_ref, c_ref, halo_ref,
           halo_send, halo_recv, pack_send, pack_recv, coef_send, coef_recv, a_send, a_recv, b_send, b_recv, result, out_sem):
    D, R, C = obs_ref.shape
    chunks = row_chunks * col_chunks
    RC, CC = R // row_chunks, C // col_chunks
    me_d, me_t = lax.axis_index("dates"), lax.axis_index("tiles")
    has_l, has_r = me_d > 0, me_d < nd - 1
    has_w, has_e = me_t > 0, me_t < nt - 1
    mask_l = jnp.where(has_l, 1.0, 0.0).astype(jnp.float32)
    mask_r = jnp.where(has_r, 1.0, 0.0).astype(jnp.float32)

    barrier = pltpu.get_barrier_semaphore()
    for o in range(1, nt):
        pl.semaphore_signal(barrier, inc=1, device_id={"tiles": lax.rem(me_t + o, nt)}, device_id_type=MESH)
    greeted = (1, nd - 1) if 2 < nd < ITERS else range(1, nd)
    for o in greeted:
        pl.semaphore_signal(barrier, inc=1, device_id={"dates": lax.rem(me_d + o, nd)}, device_id_type=MESH)

    def start_plane(t, _):
        w = mask_ref[t].astype(jnp.float32) / 3.0 + 0.05
        weights[t] = w
        basis[0, t + 2] = w * obs_ref[t]
        return 0

    edges = sorted({0, 1, D - 2, D - 1})
    for t in edges:
        start_plane(t, 0)

    pl.semaphore_wait(barrier, nt - 1 + len(greeted))

    def halo_copy(k, c, side):
        rows, cols = pl.ds(c // col_chunks * RC, RC), pl.ds(c % col_chunks * CC, CC)
        if side == 0:
            src, dst, to = basis.at[k, pl.ds(D, 2), rows, cols], basis.at[k, pl.ds(0, 2), rows, cols], me_d + 1
        else:
            src, dst, to = basis.at[k, pl.ds(2, 2), rows, cols], basis.at[k, pl.ds(D + 2, 2), rows, cols], me_d - 1
        return pltpu.make_async_remote_copy(
            src_ref=src, dst_ref=dst, send_sem=halo_send.at[k, c, side], recv_sem=halo_recv.at[k, c, side],
            device_id={"dates": to}, device_id_type=MESH)

    def pack_copy(k, side):
        return pltpu.make_async_remote_copy(
            src_ref=pack_out.at[k, side], dst_ref=pack_in.at[k, side], send_sem=pack_send.at[k, side],
            recv_sem=pack_recv.at[k, side], device_id={"tiles": me_t - 1 if side == 0 else me_t + 1}, device_id_type=MESH)

    def coef_copy(which, side):
        ref = (dr_ref, dc_ref)[which]
        cols = pl.ds(0 if side == 0 else C - LANES, LANES)
        return pltpu.make_async_remote_copy(
            src_ref=ref.at[:, cols], dst_ref=coef_in.at[side, which], send_sem=coef_send.at[side, which],
            recv_sem=coef_recv.at[side, which], device_id={"tiles": me_t - 1 if side == 0 else me_t + 1}, device_id_type=MESH)

    def send_halo(k, c, both=True):
        @pl.when(has_r)
        def _():
            halo_copy(k, c, 0).start()

        if both:
            @pl.when(has_l)
            def _():
                halo_copy(k, c, 1).start()

    def wait_halo(k, c, both=True):
        @pl.when(has_l)
        def _():
            halo_copy(k, c, 0).wait_recv()

        if both:
            @pl.when(has_r)
            def _():
                halo_copy(k, c, 1).wait_recv()

    for c in range(chunks):
        send_halo(0, c)

    @pl.when(has_w)
    def _():
        for which in range(2):
            coef_copy(which, 0).start()

    @pl.when(has_e)
    def _():
        for which in range(2):
            coef_copy(which, 1).start()

    lax.fori_loop(2, D - 2, start_plane, 0)

    def clear(ref, ks, at):
        def one(k, _):
            ref[(k,) + at] = jnp.zeros_like(ref[(k,) + at])
            return 0
        lax.fori_loop(0, ks, one, 0)

    @pl.when(jnp.logical_not(has_l))
    def _():
        clear(basis, ITERS, (pl.ds(0, 2),))

    @pl.when(jnp.logical_not(has_r))
    def _():
        clear(basis, ITERS, (pl.ds(D + 2, 2),))

    @pl.when(jnp.logical_not(has_e))
    def _():
        clear(pack_in, ITERS, (0,))
        coef_in[0] = jnp.zeros_like(coef_in[0])

    @pl.when(jnp.logical_not(has_w))
    def _():
        clear(pack_in, ITERS, (1,))
        coef_in[1] = jnp.zeros_like(coef_in[1])

    def second(v, j):
        u = v[j] - 2.0 * v[j + 1] + v[j + 2]
        if j < 0:
            u = u * mask_l
        if j >= D - 2:
            u = u * mask_r
        return u

    def next_plane(k, t, rows, cols, v, u, first):
        back = u[t - 2] - 2.0 * u[t - 1] + u[t]
        image = weights[t, rows, cols] * v[t] + smooth_weight * back
        scale = 1.0 if first else 2.0
        new = (scale / HALF) * image - (scale * MID / HALF) * v[t]
        if not first:
            new = new - basis[k - 1, t + 2, rows, cols]
        return new

    def place(c, r):
        return (pl.ds(pl.multiple_of(c // col_chunks * RC + r * SUB, SUB), SUB), pl.ds(c % col_chunks * CC, CC))

    def edge_step(k, c, first):
        def part(r, _):
            rows, cols = place(c, r)
            v, u = {}, {}
            for t in edges:
                for j in range(t - 2, t + 3):
                    if j not in v:
                        v[j] = basis[k, j + 2, rows, cols]
                for j in range(t - 2, t + 1):
                    if j not in u:
                        u[j] = second(v, j)
                basis[k + 1, t + 2, rows, cols] = next_plane(k, t, rows, cols, v, u, first)
            return 0
        if RC == SUB:
            part(0, 0)
        else:
            lax.fori_loop(0, RC // SUB, part, 0)

    def inner_step(k, c, first, last):
        def part(r, carry):
            own, cross = carry
            rows, cols = place(c, r)
            v, u = {}, {}
            for t in range(D):
                stored = t in edges
                for j in range(t - 2, t + 3):
                    if j not in v and not (stored and j != t):
                        v[j] = basis[k, j + 2, rows, cols]
                if stored:
                    new = basis[k + 1, t + 2, rows, cols]
                else:
                    for j in range(t - 2, t + 1):
                        if j not in u:
                            u[j] = second(v, j)
                    new = next_plane(k, t, rows, cols, v, u, first)
                    basis[k + 1, t + 2, rows, cols] = new
                own = own + v[t] * v[t]
                cross = cross + v[t] * new
            return own, cross

        def last_part(r, carry):
            own, energy = carry
            rows, cols = place(c, r)
            v = {j: basis[k, j + 2, rows, cols] for j in range(-2, D)}
            bend = jnp.zeros_like(own)
            for t in range(D):
                u = second(v, t - 2)
                bend = bend + u * u
                square = v[t] * v[t]
                own = own + square
                energy = energy + weights[t, rows, cols] * square
            return own, energy + smooth_weight * bend

        if last:
            part = last_part
        zero = jnp.zeros((SUB, CC), jnp.float32)
        own, cross = part(0, (zero, zero)) if RC == SUB else lax.fori_loop(0, RC // SUB, part, (zero, zero))
        for which, acc in ((0, own), (1, cross)):
            acc = functools.reduce(lambda a, b: a + b, [acc[:, i:i + LANES] for i in range(0, CC, LANES)])
            acc_ref[k, which] = acc if c == 0 else acc_ref[k, which] + acc

    lane = lax.broadcasted_iota(jnp.int32, (SUB, LANES), 1)
    group = lane // STEPS
    groups = LANES // STEPS

    def pack_step(k, c):
        def part(r, _):
            rows = pl.ds(pl.multiple_of(c * RC + r * SUB, SUB), SUB)
            west = east = jnp.zeros((SUB, LANES), jnp.float32)
            for d in range(D):
                both = jnp.where(lane < LANES // 2, basis[k, d + 2, rows, pl.ds(0, LANES)],
                                 basis[k, d + 2, rows, pl.ds(C - LANES, LANES)])
                if d:
                    both = pltpu.roll(both, STEPS * d, 1)
                west = jnp.where(group == d, both, west)
                east = jnp.where(group == (d - 1) % groups, both, east)
            pack_out[k, 0, rows] = west
            pack_out[k, 1, rows] = east
            return 0
        if RC == SUB:
            part(0, 0)
        else:
            lax.fori_loop(0, RC // SUB, part, 0)

    def send_pack(k):
        @pl.when(has_w)
        def _():
            pack_copy(k, 0).start()

        @pl.when(has_e)
        def _():
            pack_copy(k, 1).start()

    def step(k, first=False, last=False, before_last=False):
        if last:
            for c in range(row_chunks):
                pack_step(k, c)
            send_pack(k)
        for c in range(chunks):
            wait_halo(k, c, not last)
            if not last:
                edge_step(k, c, first)
                send_halo(k + 1, c, not before_last)
            inner_step(k, c, first, last)
            if not last and c % col_chunks == col_chunks - 1:
                pack_step(k, c // col_chunks)
        if not last:
            send_pack(k)

    step(0, first=True)

    def middle(k, _):
        step(k)
        return 0

    lax.fori_loop(1, ITERS - 2, middle, 0)
    step(ITERS - 2, before_last=True)
    step(ITERS - 1, last=True)

    def exchange(ref, value, axis, me, count, send, recv, meanwhile):
        ref[me] = value
        def copy(o, slot):
            return pltpu.make_async_remote_copy(
                src_ref=ref.at[me], dst_ref=ref.at[me] if slot is None else ref.at[slot],
                send_sem=send.at[o], recv_sem=recv.at[me] if slot is None else recv.at[slot],
                device_id={axis: lax.rem(me + o, count)}, device_id_type=MESH)
        for o in range(1, count):
            copy(o, None).start()
        meanwhile()
        for o in range(1, count):
            copy(o, lax.rem(me + o, count)).wait_recv()
        total = ref[0]
        for j in range(1, count):
            total = total + ref[j]
        for o in range(1, count):
            copy(o, None).wait_send()
        return total

    wide = lax.broadcasted_iota(jnp.int32, (R, LANES), 1)
    is_e, is_w = wide < STEPS, wide >= LANES - STEPS

    def ready():
        for side, has in ((0, has_e), (1, has_w)):
            @pl.when(has)
            def _():
                for which in range(2):
                    coef_copy(which, side).wait_recv()

                def one(k, _):
                    pack_copy(k, side).wait_recv()
                    return 0
                lax.fori_loop(0, ITERS, one, 0)

        def widened(ref, which):
            ends = jnp.where(is_e, coef_in[0, which], jnp.where(is_w, coef_in[1, which], 0.0))
            return jnp.concatenate([ref[...], ends], axis=1)

        dr, dc = widened(dr_ref, 0), widened(dc_ref, 1)
        row = lax.broadcasted_iota(jnp.int32, dr.shape, 0)
        coefs[0] = jnp.where(row > 0, dr, 0.0)
        coefs[1] = jnp.where(row < R - 1, dr, 0.0)
        coefs[2] = dc
        coefs[3] = 1.0 - 2.0 * dr - 2.0 * dc

    def drained():
        def sent(k, _):
            for side, has, has_t in ((0, has_r, has_w), (1, has_l, has_e)):
                @pl.when(has if side == 0 else jnp.logical_and(has, k < ITERS - 1))
                def _():
                    for c in range(chunks):
                        halo_copy(k, c, side).wait_send()

                @pl.when(has_t)
                def _():
                    pack_copy(k, side).wait_send()
            return 0

        lax.fori_loop(0, ITERS, sent, 0)
        for side, has in ((0, has_w), (1, has_e)):
            @pl.when(has)
            def _():
                for which in range(2):
                    coef_copy(which, side).wait_send()

    n_mom = 2 * ITERS
    mine = jnp.sum(acc_ref[...].reshape(n_mom, SUB, LANES), axis=1)
    mine = jnp.concatenate([mine, jnp.zeros((sum_a.shape[1] - n_mom, LANES), jnp.float32)], axis=0)
    total = exchange(sum_a, mine, "tiles", me_t, nt, a_send, a_recv, ready)
    total = exchange(sum_b, total, "dates", me_d, nd, b_send, b_recv, drained)
    nu_ref[...] = jnp.broadcast_to(jnp.sum(total, axis=1, keepdims=True), nu_ref.shape)

    raw = [jnp.broadcast_to(nu_ref[j:j + 1, :], (SUB, LANES)) for j in range(n_mom)]
    unit = 1.0 / raw[0]
    raw = [value * unit for value in raw]
    raw[-1] = (2.0 / HALF) * (raw[-1] - MID * raw[-2]) - raw[-3]
    nu = raw[:2]
    for k in range(1, ITERS):
        nu += [2.0 * raw[2 * k] - nu[0], 2.0 * raw[2 * k + 1] - nu[1]]
    h = [MID * nu[m] + (HALF * 0.5) * (nu[m + 1] + nu[abs(m - 1)]) for m in range(n_mom - 1)]
    M = {(i, j): 0.5 * (h[i + j] + h[j - i]) for i in range(ITERS) for j in range(i, ITERS)}
    b = list(nu[:ITERS])
    size = [M[i, i] for i in range(ITERS)]
    inverse, worst = [], None
    for i in range(ITERS):
        inverse.append(1.0 / M[i, i])
        ratio = jnp.where(M[i, i] > PIVOT_MIN * size[i], 1.0, 0.0)
        worst = ratio if worst is None else worst * ratio
        for j in range(i + 1, ITERS):
            f = M[i, j] * inverse[i]
            for q in range(j, ITERS):
                M[j, q] = M[j, q] - f * M[i, q]
            b[j] = b[j] - f * b[i]
    coef = [None] * ITERS
    for i in reversed(range(ITERS)):
        s = b[i]
        for q in range(i + 1, ITERS):
            s = s - M[i, q] * coef[q]
        coef[i] = s * inverse[i]
        c_ref[i] = coef[i]
    flag_ref[0] = jnp.min(worst)

    cs = [c_ref[i, 0:1, :] for i in range(ITERS)]
    for side in range(2):
        halo_ref[side] = functools.reduce(lambda a, b: a + b, [cs[i] * pack_in[i, side] for i in range(ITERS)])

    width = C + LANES

    def diffuse(d, _):
        parts = []
        for i in range(0, C, LANES):
            parts.append(functools.reduce(
                lambda a, b: a + b, [c_ref[k, 0:1, :] * basis[k, d + 2, :, pl.ds(i, LANES)] for k in range(ITERS)]))
        ends = jnp.where(wide // STEPS == d, halo_ref[0], halo_ref[1])
        ends = pltpu.roll(ends, lax.rem(LANES - STEPS * d, LANES), 1)
        parts.append(jnp.where(jnp.logical_or(is_e, is_w), ends, 0.0))
        f = jnp.concatenate(parts, axis=1)
        for _ in range(STEPS):
            f = (coefs[3] * f + coefs[0] * pltpu.roll(f, 1, 0) + coefs[1] * pltpu.roll(f, R - 1, 0)
                 + coefs[2] * (pltpu.roll(f, 1, 1) + pltpu.roll(f, width - 1, 1)))
        result[d] = f[:, :C]
        return 0

    some = D // 4 if D % 16 == 0 else D
    leaving = []
    for at in range(0, D, some):
        lax.fori_loop(at, at + some, diffuse, 0, unroll=4 if D * R <= 1024 else 1)
        leaving.append(pltpu.make_async_copy(
            result.at[pl.ds(at, some)], out_ref.at[pl.ds(at, some)], out_sem.at[at // some]))
        leaving[-1].start()
    for copy in leaving:
        copy.wait()


def fast(nd, nt, observed, cloud_mask, diffuse_rows, diffuse_cols):
    D, R, C = observed.shape
    row_chunks, col_chunks = 4, 1
    chunks = row_chunks * col_chunks
    slots = 24
    f32 = jnp.float32
    DMA = pltpu.SemaphoreType.DMA
    V = pl.BlockSpec(memory_space=pltpu.VMEM)
    return pl.pallas_call(
        functools.partial(kernel, nd, nt, row_chunks, col_chunks),
        out_shape=(jax.ShapeDtypeStruct((D, R, C), f32), jax.ShapeDtypeStruct((1,), f32)),
        in_specs=[V] * 4,
        out_specs=(pl.BlockSpec(memory_space=pl.ANY), pl.BlockSpec(memory_space=pltpu.SMEM)),
        scratch_shapes=[
            pltpu.VMEM((ITERS, D + 4, R, C), f32),
            pltpu.VMEM((D, R, C), f32),
            pltpu.VMEM((ITERS, 2, R, LANES), f32),
            pltpu.VMEM((ITERS, 2, R, LANES), f32),
            pltpu.VMEM((2, 2, R, LANES), f32),
            pltpu.VMEM((4, R, C + LANES), f32),
            pltpu.VMEM((ITERS, 2, SUB, LANES), f32),
            pltpu.VMEM((nt, slots, LANES), f32),
            pltpu.VMEM((nd, slots, LANES), f32),
            pltpu.VMEM((slots, LANES), f32),
            pltpu.VMEM((ITERS, SUB, LANES), f32),
            pltpu.VMEM((2, R, LANES), f32),
            DMA((ITERS, chunks, 2)), DMA((ITERS, chunks, 2)),
            DMA((ITERS, 2)), DMA((ITERS, 2)),
            DMA((2, 2)), DMA((2, 2)),
            DMA((nt,)), DMA((nt,)),
            DMA((nd,)), DMA((nd,)),
            pltpu.VMEM((D, R, C), f32), DMA((4,)),
        ],
        compiler_params=pltpu.CompilerParams(
            collective_id=0, has_side_effects=True, vmem_limit_bytes=60 * 1024 * 1024),
        name="smooth_and_fill",
    )(observed, cloud_mask, diffuse_rows, diffuse_cols)


def padded_by(cells, axis, dim, width):
    count = lax.axis_size(axis)
    head = lax.slice_in_dim(cells, 0, width, axis=dim)
    tail = lax.slice_in_dim(cells, cells.shape[dim] - width, cells.shape[dim], axis=dim)
    return jnp.concatenate(
        [
            lax.ppermute(tail, axis, [(i, i + 1) for i in range(count - 1)]),
            cells,
            lax.ppermute(head, axis, [(i + 1, i) for i in range(count - 1)]),
        ],
        axis=dim,
    )


def total_of(value):
    for axis in ("tiles", "dates"):
        count = lax.axis_size(axis)
        shift = 1
        while shift < count:
            value = value + lax.ppermute(value, axis, [(i, i ^ shift) for i in range(count)])
            shift *= 2
    return value


def plain(observed, cloud_mask, diffuse_rows, diffuse_cols):
    weights = cloud_mask.astype(jnp.float32) / 3.0 + 0.05
    rhs = weights * observed
    D = rhs.shape[0]
    dates = D * lax.axis_size("dates")
    place = lax.axis_index("dates") * D - 2 + jnp.arange(D + 2)
    inside = jnp.logical_and(place >= 0, place < dates - 2)[:, None, None]

    def time_operator(values):
        wide = padded_by(values, "dates", 0, 2)
        second = jnp.where(inside, wide[:-2] - 2.0 * wide[1:-1] + wide[2:], 0.0)
        return weights * values + smooth_weight * (second[:-2] - 2.0 * second[1:-1] + second[2:])

    def advance(step, state):
        smoothed, residual, direction, norm_now = state
        image = time_operator(direction)
        alpha = norm_now / total_of(jnp.sum(direction * image))
        smoothed = smoothed + alpha * direction
        residual = residual - alpha * image
        fresh = total_of(jnp.sum(residual * residual))
        direction = residual + fresh / norm_now * direction
        return (smoothed, residual, direction, fresh)

    state = (jnp.zeros_like(rhs), rhs, rhs, total_of(jnp.sum(rhs * rhs)))
    filled = lax.fori_loop(0, ITERS, advance, state)[0]

    def spread(step, filled):
        padded = jnp.pad(padded_by(filled, "tiles", 2, 1), ((0, 0), (1, 1), (0, 0)))
        centre = padded[:, 1:-1, 1:-1]
        along_rows = padded[:, 2:, 1:-1] + padded[:, :-2, 1:-1] - 2.0 * centre
        along_cols = padded[:, 1:-1, 2:] + padded[:, 1:-1, :-2] - 2.0 * centre
        return filled + diffuse_rows * along_rows + diffuse_cols * along_cols

    return lax.fori_loop(0, STEPS, spread, filled)


def solution(mesh):
    nd, nt = mesh.shape["dates"], mesh.shape["tiles"]

    def body(observed, cloud_mask, diffuse_rows, diffuse_cols):
        filled, good = fast(nd, nt, observed, cloud_mask, diffuse_rows, diffuse_cols)
        return lax.cond(
            good[0] > 0.5,
            lambda: filled,
            lambda: plain(observed, cloud_mask, diffuse_rows, diffuse_cols),
        )

    in_specs = (
        P("dates", None, "tiles"),
        P("dates", None, "tiles"),
        P(None, "tiles"),
        P(None, "tiles"),
    )
    return jax.shard_map(body, mesh=mesh, in_specs=in_specs, out_specs=P("dates", None, "tiles"), check_vma=False)
```
